768 devices in a mesh: src: 12 (over x, z_lo), rcv: 64 (over z_hi, y, core).
Axes of the slice: x: 4, y: 8, z: 12 (z_hi: 4, z_lo: 3; z = z_hi * 3 + z_lo), core: 2. Of those that a mesh axis runs over, the one named last changes fastest.
Arguments:
- record: bfloat16 [1, 2, 6144, 6144], P(None, None, 'rcv', 'src'), may hold values from -6 to 6
- panel_offset: int32 [768], replicated, may hold values from 0 to 7
Outputs:
- primaries: bfloat16 [1, 2, 6144, 6144], P(None, None, 'rcv', 'src')
- multiples: bfloat16 [1, 2, 6144, 6144], P(None, None, 'rcv', 'src')
The draws below stay inside these ranges and needn't reach their ends.
Inputs may be any that keep to these rules, and one draw needn't show every extreme that they name: Panel station j is 8 * j + panel_offset[j].
All inputs are finite; a program needn't handle non-finite values.
Results may differ from the reference program's by a relative error of at most 0.003.
The reference program's roundings to bfloat16 on the way count: a program that leaves them out, or rounds other values in their place, can miss the bound.
Values may be sent and summed in bfloat16 or wider, within the bound.
No kernel may reach another device: no remote copies, remote signals or barrier semaphores. Data moves between devices by JAX's collectives and lax.ppermute only.
A program may use at most 32 MiB of HBM per device.

```python
import jax
import jax.numpy as jnp
from jax import lax

NFREQ = 1
NSTA = 6144
STRIDE = 8
REACH = 4
SWEEPS = 2
PANEL = 768
N_SRC = 12
N_RCV = 64


def with_ends(entries, key, least, largest):
    spot = [jax.random.randint(jax.random.fold_in(key, axis), (), 0, length) for axis, length in enumerate(entries.shape)]
    longest = entries.shape.index(max(entries.shape))
    neighbour = spot[:longest] + [(spot[longest] + 1) % entries.shape[longest]] + spot[longest + 1:]
    return entries.at[tuple(spot)].set(least).at[tuple(neighbour)].set(largest)


def level_of(stream_key, extent, split, smallest, largest):
    gain, own = 1.0, jax.random.fold_in(stream_key, 6)
    for position, shards_of in split:
        draws = jnp.exp(jax.random.uniform(jax.random.fold_in(own, position), (shards_of,), jnp.float32, smallest / len(split), largest / len(split)))
        gain = gain * jnp.repeat(draws, extent[position] // shards_of).reshape([-1 if axis == position else 1 for axis in range(len(extent))])
    return gain


def normal_values(rng, dims, scale, limit, pieces=(), kind=jnp.bfloat16):
    result = jax.random.normal(rng, dims, jnp.float32) * scale
    if len(pieces) > 0:
        result = level_of(rng, dims, pieces, -0.22, 0.18) * result
    return jnp.clip(result, min=-limit, max=limit).astype(kind)


def setup_inputs(seed: int = 0) -> dict:
    arg_keys = jax.random.split(jax.random.key(seed), 3)
    return {
        "record": normal_values(arg_keys[0], (NFREQ, 2, NSTA, NSTA), 1.0, 6.0, ((2, 64), (3, 12))),
        "panel_offset": with_ends(jax.random.randint(arg_keys[1], (PANEL,), 0, STRIDE), jax.random.fold_in(arg_keys[1], 1), 0, STRIDE - 1).astype(jnp.int32),
    }


weight_eps = 1e-6


def box_total(values):
    rows_recv = values.shape[0]
    rows_source = values.shape[1]
    padded = jnp.pad(values, ((REACH, REACH), (REACH, REACH)))
    recv_total = padded[0:rows_recv, :]
    for shift_pos in range(1, 2 * REACH + 1):
        recv_total = recv_total + padded[shift_pos:shift_pos + rows_recv, :]
    box_totals = recv_total[:, 0:rows_source]
    for shift_pos in range(1, 2 * REACH + 1):
        box_totals = box_totals + recv_total[:, shift_pos:shift_pos + rows_source]
    return box_totals


def reference(record, panel_offset):
    stations = record.shape[2]
    src_rows = stations // N_SRC
    rcv_cols = stations // N_RCV
    run_len = stations // (N_SRC * N_RCV)
    station = jnp.arange(stations, dtype=jnp.int32)
    column_of = rcv_cols * ((station % src_rows) // run_len) + run_len * (station // src_rows) + station % run_len
    station_of = src_rows * ((station % rcv_cols) // run_len) + run_len * (station // rcv_cols) + station % run_len
    natural = jnp.take(record, column_of.astype(jnp.int32), axis=2)
    keys = (STRIDE * jnp.arange(PANEL, dtype=jnp.int32) + panel_offset).astype(jnp.int32)
    front = jnp.swapaxes(jnp.take(natural, keys, axis=2), 2, 3)
    behind = jnp.take(natural, keys, axis=3)
    symmetric = ((front.astype(jnp.float32) + behind.astype(jnp.float32)) * 0.5).astype(jnp.bfloat16)
    prim_list = []
    mult_list = []
    for freq_index in range(NFREQ):
        real_part = symmetric[freq_index, 0]
        imag_part = symmetric[freq_index, 1]
        pred_real = jnp.dot(real_part, real_part.T, preferred_element_type=jnp.float32) - jnp.dot(imag_part, imag_part.T, preferred_element_type=jnp.float32)
        pred_imag = jnp.dot(real_part, imag_part.T, preferred_element_type=jnp.float32) + jnp.dot(imag_part, real_part.T, preferred_element_type=jnp.float32)
        round_real = lax.optimization_barrier(pred_real.astype(jnp.bfloat16)).astype(jnp.float32)
        round_imag = lax.optimization_barrier(pred_imag.astype(jnp.bfloat16)).astype(jnp.float32)
        data_real = natural[freq_index, 0].astype(jnp.float32)
        data_imag = natural[freq_index, 1].astype(jnp.float32)
        err_real = data_real
        err_imag = data_imag
        for sweep_step in range(SWEEPS):
            weight = 1.5 - jnp.tanh(err_real * err_real + err_imag * err_imag)
            num_real = box_total(weight * (round_real * data_real + round_imag * data_imag))
            num_imag = box_total(weight * (round_real * data_imag - round_imag * data_real))
            denom = box_total(weight * (round_real * round_real + round_imag * round_imag)) + weight_eps
            gain_real = num_real / denom
            gain_imag = num_imag / denom
            err_real = data_real - (gain_real * round_real - gain_imag * round_imag)
            err_imag = data_imag - (gain_real * round_imag + gain_imag * round_real)
        prim_list.append(jnp.stack([err_real, err_imag]))
        mult_list.append(jnp.stack([pred_real, pred_imag]) * (PANEL ** -0.5))
    primaries = jnp.take(jnp.stack(prim_list), station_of.astype(jnp.int32), axis=2).astype(jnp.bfloat16)
    multiples = jnp.take(jnp.stack(mult_list), station_of.astype(jnp.int32), axis=2).astype(jnp.bfloat16)
    return primaries, multiples
```

```python
import jax
import jax.numpy as jnp
from jax import lax
from jax.experimental import pallas as pl
from jax.experimental.pallas import tpu as pltpu
from jax.sharding import PartitionSpec as P

NZ, NY, NC = 4, 8, 2
NP = NY * NC
NA = 12
TILES = 3 * NZ
EXT = 640
STRIDE = 8
REACH = 4
EPS = 1e-6
F32, BF16 = jnp.float32, jnp.bfloat16


def vmem(count):
    return [pl.BlockSpec(memory_space=pltpu.VMEM)] * count


def smem(count):
    return [pl.BlockSpec(memory_space=pltpu.SMEM)] * count


def pick_kernel(pos, panel, rec, to_rcv, to_src):
    src, rcv = pos[0], pos[1]
    lane = lax.broadcasted_iota(jnp.int32, (1, 128), 1)
    slot = lane % 8
    key_part, key_pos = slot // 4, 16 * (slot % 4) + lane // 8
    offset = jnp.zeros((1, 128), jnp.int32)
    for g in range(64):
        offset = jnp.where(key_pos == g, panel[64 * src + g], offset)
    key_row = STRIDE * key_pos + offset
    rows = lax.broadcasted_iota(jnp.int32, (512, 128), 0)
    total = jnp.zeros((96, 128), F32)
    for part in range(2):
        chosen = ((rows == key_row) & (key_part == part)).astype(F32).astype(BF16)
        total += jnp.dot(rec[part], chosen, preferred_element_type=F32)
    to_src[...] = total.astype(BF16).reshape(NA, 8, 128)
    run, run_part, run_z = (lane % 32) // 2, lane % 2, lane // 32
    offset = jnp.zeros((1, 128), jnp.int32)
    for a in range(NA):
        offset = jnp.where(run == a, panel[64 * a + rcv], offset)
    col = jnp.where(run < NA, STRIDE * run + offset, -1)
    rows = lax.broadcasted_iota(jnp.int32, (96, 128), 0)
    total = jnp.zeros((128, 128), F32)
    for z in range(NZ):
        for part in range(2):
            chosen = ((rows == col) & (run_part == part) & (run_z == z)).astype(F32).astype(BF16)
            total += lax.dot_general(
                rec[part, :, 128 * z : 128 * z + 128],
                chosen,
                (((0,), (0,)), ((), ())),
                preferred_element_type=F32,
            )
    to_rcv[...] = total.astype(BF16).reshape(NP, 8, 128)


def order_kernel(from_rcv, from_src, out):
    lane = lax.broadcasted_iota(jnp.int32, (8, 128), 1)
    rcv_tiles = [from_rcv[p].astype(F32) for p in range(NP)]
    tiles = []
    for z in range(NZ):
        for third in range(3):
            acc = jnp.zeros((8, 128), F32)
            for p in range(NP):
                shift = (8 * p - 32 * z - 8 * third) % 128
                moved = pltpu.roll(rcv_tiles[p], shift, 1) if shift else rcv_tiles[p]
                acc = jnp.where(lane // 8 == p, moved, acc)
            tiles.append(acc)
    src_tiles = [from_src[a].astype(F32) for a in range(NA)]
    for z in range(NZ):
        for third in range(3):
            acc = jnp.zeros((8, 128), F32)
            for j in range(8):
                shift = (j - (4 * (j % 2) + z)) % 128
                tile = src_tiles[4 * third + j // 2]
                moved = pltpu.roll(tile, shift, 1) if shift else tile
                acc = jnp.where(lane % 8 == j, moved, acc)
            tiles.append(acc)
    for n, tile in enumerate(tiles):
        tile = tile.astype(BF16)
        for z in range(NZ):
            out[z, n] = tile


def average_kernel(pos, pieces, rows, own):
    for z in range(NZ):
        for tile in range(TILES):
            front = pieces[tile // 3, 3 * z + tile % 3].astype(F32)
            behind = pieces[z, TILES + tile].astype(F32)
            rows[z, tile] = ((front + behind) * 0.5).astype(BF16)
    own[...] = rows[pos[1] // NP]


def windows_rows(x, count):
    two = x[:-1] + x[1:]
    four = two[:-2] + two[2:]
    eight = four[:-4] + four[4:]
    return eight[:count] + x[8 : 8 + count]


def windows_lanes(x):
    two = x + pltpu.roll(x, EXT - 1, 1)
    four = two + pltpu.roll(two, EXT - 2, 1)
    eight = four + pltpu.roll(four, EXT - 4, 1)
    return pltpu.roll(eight + pltpu.roll(x, EXT - 8, 1), 4, 1)


def final_kernel(pos, rec, rec_lo, rec_hi, sr, sr_lo, sr_hi, ss, sp, row_hi, row_lo, prim, mult, a_re, a_im, b_rows, pred):
    rcv = pos[1]
    core = rcv % 2
    first, last = (rcv == 0).astype(jnp.int32), (rcv == NZ * NP - 1).astype(jnp.int32)
    lane = lax.broadcasted_iota(jnp.int32, (24, 128), 1)
    even = lane % 2 == 0

    def spread(a, _):
        lo, hi = jnp.maximum(a - first, 0), jnp.minimum(a + last, NA - 1)
        keep_lo = (a - first >= 0).astype(F32)
        keep_hi = (a + last <= NA - 1).astype(F32)
        for t in range(TILES):
            x = jnp.concatenate(
                [sr_lo[lo, t].astype(F32) * keep_lo, sr[a, t].astype(F32), sr_hi[hi, t].astype(F32) * keep_hi], axis=0
            )
            a_re[a, :, 128 * t : 128 * t + 128] = jnp.where(even, x, -x)
            a_im[a, :, 128 * t : 128 * t + 128] = jnp.where(even, pltpu.roll(x, 127, 1), pltpu.roll(x, 1, 1))
        return 0

    lax.fori_loop(0, NA, spread, 0)

    def gather(z, _):
        for t in range(TILES):
            mine, theirs = ss[:, z, t].astype(F32), sp[:, z, t].astype(F32)
            zero = jnp.where(core == 0, mine, theirs)
            one = jnp.where(core == 0, theirs, mine)
            x = jnp.stack([zero, one], axis=1).reshape(128, 128)
            b_rows[z, :, 128 * t : 128 * t + 128] = x.astype(BF16)
        return 0

    lax.fori_loop(0, NZ, gather, 0)
    for t in range(TILES):
        x = jnp.concatenate([row_hi[t].astype(F32), jnp.zeros((112, 128), F32), row_lo[t].astype(F32)], axis=0)
        b_rows[NZ, :, 128 * t : 128 * t + 128] = x.astype(BF16)
    left_re = a_re[...].reshape(24 * NA, 128 * TILES).astype(BF16)
    left_im = a_im[...].reshape(24 * NA, 128 * TILES).astype(BF16)
    for n in range(NZ + 1):
        right = b_rows[n]
        for part, left in enumerate((left_re, left_im)):
            value = lax.dot_general(left, right, (((1,), (1,)), ((), ())), preferred_element_type=F32)
            pred[part, :, :, 128 * n : 128 * n + 128] = value.reshape(NA, 24, 128)

    def sweep(a, _):
        lo, hi = jnp.maximum(a - first, 0), jnp.minimum(a + last, NA - 1)
        keep_lo = (a - first >= 0).astype(F32)
        keep_hi = (a + last <= NA - 1).astype(F32)
        data, guess = [], []
        for part in range(2):
            data.append(
                jnp.concatenate(
                    [rec_lo[part, lo].astype(F32) * keep_lo, rec[part, a].astype(F32), rec_hi[part, hi].astype(F32) * keep_hi],
                    axis=0,
                )
            )
            full = pred[part, a]
            mult[part, a] = (full[8:16, :512] * (768.0 ** -0.5)).astype(BF16)
            guess.append(full.astype(BF16).astype(F32))
        dr, di = data
        pr, pi = guess
        terms = [pr * dr + pi * di, pr * di - pi * dr, pr * pr + pi * pi]
        weight = 1.5 - jnp.tanh(dr * dr + di * di)
        num_re, num_im, den = [windows_lanes(windows_rows(weight * q, 16)) for q in terms]
        den = den + EPS
        gain_re, gain_im = num_re / den, num_im / den
        dr, di, pr, pi = [v[4:20] for v in (dr, di, pr, pi)]
        er = dr - (gain_re * pr - gain_im * pi)
        ei = di - (gain_re * pi + gain_im * pr)
        weight = 1.5 - jnp.tanh(er * er + ei * ei)
        num_re, num_im, den = [windows_lanes(windows_rows(weight * q[4:20], 8)) for q in terms]
        den = den + EPS
        gain_re, gain_im = num_re / den, num_im / den
        dr, di, pr, pi = [v[4:12] for v in (dr, di, pr, pi)]
        prim[0, a] = (dr - (gain_re * pr - gain_im * pi))[:, :512].astype(BF16)
        prim[1, a] = (di - (gain_re * pi + gain_im * pr))[:, :512].astype(BF16)
        return 0

    lax.fori_loop(0, NA, sweep, 0)


def shape(*dims):
    return jax.ShapeDtypeStruct(dims, BF16)


def ring(count, step, closed):
    return [(n, (n + step) % count) for n in range(count) if closed or 0 <= n + step < count]


def shards(record, panel_offset):
    src_count, rcv_count = lax.axis_size("src"), lax.axis_size("rcv")
    src, rcv = lax.axis_index("src"), lax.axis_index("rcv")
    pos = jnp.stack([src, rcv]).astype(jnp.int32)
    rec = record[0]
    plane = [[z * NP + p for p in range(NP)] for z in range(NZ)]
    column = [[z * NP + p for z in range(NZ)] for p in range(NP)]
    line = [[z * NP + y * NC + c for y in range(NY)] for z in range(NZ) for c in range(NC)]
    swap = [(n, n ^ 1) for n in range(rcv_count)]

    def exchange(x, axis, groups=None):
        return lax.all_to_all(x, axis, split_axis=0, concat_axis=0, tiled=True, axis_index_groups=groups)

    def copies(x, count, axis, groups=None):
        return exchange(jnp.broadcast_to(x, (count, *x.shape)), axis, groups)

    next_src = lax.ppermute(rec[:, :, :128], "src", ring(src_count, -1, False))
    last_src = lax.ppermute(rec[:, :, 384:], "src", ring(src_count, 1, False))
    lane = lax.broadcasted_iota(jnp.int32, (1, 1, 128), 2)
    rim = jnp.where(lane < 8, next_src, jnp.where(lane >= 120, last_src, jnp.zeros_like(last_src)))
    wide = jnp.concatenate([rec, rim], axis=2).reshape(2, NA, 8, EXT)
    wide_lo = lax.ppermute(wide, "rcv", ring(rcv_count, 1, True))
    wide_hi = lax.ppermute(wide, "rcv", ring(rcv_count, -1, True))

    to_rcv, to_src = pl.pallas_call(
        pick_kernel,
        out_shape=(shape(NP, 8, 128), shape(NA, 8, 128)),
        in_specs=smem(2) + vmem(1),
        out_specs=vmem(2),
    )(pos, panel_offset, rec)
    from_src = exchange(to_src, "src")
    from_rcv = exchange(to_rcv, "rcv", plane)
    message = pl.pallas_call(
        order_kernel, out_shape=shape(NZ, 2 * TILES, 8, 128), in_specs=vmem(2), out_specs=vmem(1)[0]
    )(from_rcv, from_src)
    pieces = exchange(message, "rcv", column)
    rows, own = pl.pallas_call(
        average_kernel,
        out_shape=(shape(NZ, TILES, 8, 128), shape(TILES, 8, 128)),
        in_specs=smem(1) + vmem(1),
        out_specs=vmem(2),
    )(pos, pieces)
    sr = copies(own, src_count, "src")
    ss = copies(rows, NY, "rcv", line)
    sr_lo = lax.ppermute(sr, "rcv", ring(rcv_count, 1, True))
    sr_hi = lax.ppermute(sr, "rcv", ring(rcv_count, -1, True))
    sp = lax.ppermute(ss, "rcv", swap)
    even_core = rcv % 2 == 0
    row_first = jnp.where(even_core, ss[0, 0], sp[0, 0])
    row_last = jnp.where(even_core, sp[NY - 1, NZ - 1], ss[NY - 1, NZ - 1])
    row_hi = lax.ppermute(row_first, "src", ring(src_count, -1, False))
    row_lo = lax.ppermute(row_last, "src", ring(src_count, 1, False))
    prim, mult = pl.pallas_call(
        final_kernel,
        out_shape=(shape(2, NA, 8, 512), shape(2, NA, 8, 512)),
        in_specs=smem(1) + vmem(10),
        out_specs=vmem(2),
        scratch_shapes=[
            pltpu.VMEM((NA, 24, 128 * TILES), F32),
            pltpu.VMEM((NA, 24, 128 * TILES), F32),
            pltpu.VMEM((NZ + 1, 128, 128 * TILES), BF16),
            pltpu.VMEM((2, NA, 24, EXT), F32),
        ],
    )(pos, wide, wide_lo, wide_hi, sr, sr_lo, sr_hi, ss, sp, row_hi, row_lo)
    return prim.reshape(record.shape), mult.reshape(record.shape)


def solution(mesh):
    in_specs = (P(None, None, "rcv", "src"), P())
    out_specs = (P(None, None, "rcv", "src"), P(None, None, "rcv", "src"))
    return jax.shard_map(shards, mesh=mesh, in_specs=in_specs, out_specs=out_specs, check_vma=False)
```

```python
import jax
import jax.numpy as jnp
from jax import lax
from jax.experimental import pallas as pl
from jax.experimental.pallas import tpu as pltpu
from jax.sharding import PartitionSpec as P

NZ, NY, NC = 4, 8, 2
NP = NY * NC
NA = 12
TILES = 3 * NZ
EXT = 640
STRIDE = 8
REACH = 4
EPS = 1e-6
F32, BF16 = jnp.float32, jnp.bfloat16


def vmem(count):
    return [pl.BlockSpec(memory_space=pltpu.VMEM)] * count


def smem(count):
    return [pl.BlockSpec(memory_space=pltpu.SMEM)] * count


def pick_behind_kernel(pos, panel, rec, to_src):
    lane = lax.broadcasted_iota(jnp.int32, (1, 128), 1)
    early = pos[0] < 8
    key_part = jnp.where(early, lane % 8 // 4, lane // 64)
    key_pos = 16 * (lane % 4) + jnp.where(early, lane // 8, lane % 64 // 4)
    offset = jnp.zeros((1, 128), jnp.int32)
    for g in range(64):
        offset = jnp.where(key_pos == g, panel[64 * pos[0] + g], offset)
    key_row = STRIDE * key_pos + offset
    rows = lax.broadcasted_iota(jnp.int32, (512, 128), 0)
    total = jnp.zeros((96, 128), F32)
    for part in range(2):
        chosen = ((rows == key_row) & (key_part == part)).astype(F32).astype(BF16)
        total += jnp.dot(rec[part], chosen, preferred_element_type=F32)
    to_src[...] = total.astype(BF16).reshape(NA, 8, 128)


def pick_front_kernel(pos, panel, rec, to_rcv):
    lane = lax.broadcasted_iota(jnp.int32, (1, 128), 1)
    kind, slot, run_z = lane % 32 // 8, lane % 8, lane // 32
    run = jnp.where(kind < 2, slot, jnp.where(kind == 2, 8 + slot % 4, NA))
    run_part = jnp.where(kind < 2, kind, slot // 4)
    offset = jnp.zeros((1, 128), jnp.int32)
    for a in range(NA):
        offset = jnp.where(run == a, panel[64 * a + pos[1]], offset)
    col = jnp.where(run < NA, STRIDE * run + offset, -1)
    rows = lax.broadcasted_iota(jnp.int32, (96, 128), 0)
    total = jnp.zeros((128, 128), F32)
    for z in range(NZ):
        for part in range(2):
            chosen = ((rows == col) & (run_part == part) & (run_z == z)).astype(F32).astype(BF16)
            total += lax.dot_general(
                rec[part, :, 128 * z : 128 * z + 128],
                chosen,
                (((0,), (0,)), ((), ())),
                preferred_element_type=F32,
            )
    to_rcv[...] = total.astype(BF16).reshape(NP, 8, 128)


def turned(x, shift):
    return pltpu.roll(x, shift % 128, 1) if shift % 128 else x


def order_behind_kernel(from_src, behind):
    lane = lax.broadcasted_iota(jnp.int32, (8, 128), 1)
    tiles = [from_src[a].astype(F32) for a in range(NA)]
    for part in range(2):
        for pair in range(2):
            for kind in range(2):
                acc = jnp.zeros((8, 128), F32)
                for a in range(8):
                    acc = jnp.where(lane % 8 == a, turned(tiles[a], a - (4 * part + 2 * pair + kind)), acc)
                behind[6 * part + 3 * pair + kind] = acc.astype(BF16)
            acc = jnp.zeros((8, 128), F32)
            for odd in range(2):
                for a in range(8, NA):
                    shift = 64 * (odd - part) + a - 8 - (2 * pair + odd)
                    acc = jnp.where((lane // 64 == odd) & (lane % 4 == a - 8), turned(tiles[a], shift), acc)
            behind[6 * part + 3 * pair + 2] = acc.astype(BF16)


def order_kernel(pos, from_rcv, behind, out):
    lane = lax.broadcasted_iota(jnp.int32, (8, 128), 1)
    tiles = [from_rcv[p].astype(F32) for p in range(NP)]
    odd = pos[1] // NP % 2 == 1
    for z in range(NZ):
        for kind in range(3):
            acc = jnp.zeros((8, 128), F32)
            for p in range(NP):
                if kind < 2:
                    acc = jnp.where(lane // 8 == p, turned(tiles[p], 8 * p - 32 * z - 8 * kind), acc)
                else:
                    for part in range(2):
                        shift = 64 * part + 4 * p - 32 * z - 16 - 4 * part
                        acc = jnp.where(lane // 4 == 16 * part + p, turned(tiles[p], shift), acc)
            if kind == 2:
                acc = jnp.where(odd, pltpu.roll(acc, 64, 1), acc)
            tile = acc.astype(BF16)
            for copy in range(NZ):
                out[copy, 3 * z + kind] = tile
    for copy in range(NZ):
        out[copy, TILES:] = behind[...]


def average_kernel(pos, pieces, rows, own):
    low = lax.broadcasted_iota(jnp.int32, (8, 128), 1) < 64
    for z in range(NZ):
        for tile in range(TILES):
            part, pair, kind = tile // 6, tile % 6 // 3, tile % 3
            if kind < 2:
                front = pieces[2 * pair + kind, 3 * z + part].astype(F32)
            else:
                even, odd = [pieces[2 * pair + n, 3 * z + 2].astype(F32) for n in range(2)]
                front = pltpu.roll(jnp.where(low, odd, even), 64, 1) if part else jnp.where(low, even, odd)
            rows[z, tile] = ((front + pieces[z, TILES + tile].astype(F32)) * 0.5).astype(BF16)
    own[...] = rows[pos[1] // NP]


def bounds(rcv):
    return (rcv == 0).astype(jnp.int32), (rcv == NZ * NP - 1).astype(jnp.int32)


def sides(core, partner, beyond):
    return jnp.where(core == 0, beyond, partner), jnp.where(core == 0, partner, beyond)


def neighbours(a, first, last):
    keep_lo = (a - first >= 0).astype(F32)
    keep_hi = (a + last <= NA - 1).astype(F32)
    return jnp.maximum(a - first, 0), jnp.minimum(a + last, NA - 1), keep_lo, keep_hi


def windows_rows(x, count):
    two = x[:-1] + x[1:]
    four = two[:-2] + two[2:]
    eight = four[:-4] + four[4:]
    return eight[:count] + x[8 : 8 + count]


def windows_lanes(source, target, band, pairs):
    count = EXT // 128
    rows = source.shape[0] * source.shape[1] * source.shape[2]
    tiles = []
    for n in range(count):
        x = source[:, :, :, 128 * n : 128 * n + 128].reshape(rows, 128)
        high = x.astype(BF16)
        tiles.append((high, (x - high.astype(F32)).astype(BF16)))
    for n in pairs:
        width = min(2, count - n)
        total = jnp.zeros((rows, 128 * width), F32)
        for half in range(2):
            near = jnp.concatenate([tiles[(n + m) % count][half] for m in range(-1, width + 1)], axis=1)
            total += jnp.dot(near, band[: 128 * (width + 2), : 128 * width], preferred_element_type=F32)
        target[:, :, :, 128 * n : 128 * (n + width)] = total.reshape(*target.shape[:3], 128 * width)


def final_kernel(pos, rec, rec_partner, rec_beyond, sr, ss, sp, row_hi, row_lo, prim, mult, a_rows, b_rows, pred, once, box):
    rcv = pos[1]
    core = rcv % 2
    first, last = bounds(rcv)

    def gather(z, _):
        for t in range(TILES):
            mine, theirs = ss[:, z, t].astype(F32), sp[:, z, t].astype(F32)
            zero = jnp.where(core == 0, mine, theirs)
            one = jnp.where(core == 0, theirs, mine)
            x = jnp.stack([zero, one], axis=1).reshape(128, 128)
            b_rows[z, :, 128 * t : 128 * t + 128] = x.astype(BF16)
        return 0

    lax.fori_loop(0, NZ, gather, 0)
    for t in range(TILES):
        x = jnp.concatenate([row_hi[t].astype(F32), jnp.zeros((112, 128), F32), row_lo[t].astype(F32)], axis=0)
        b_rows[NZ, :, 128 * t : 128 * t + 128] = x.astype(BF16)

    def spread(a, _):
        lo, hi, keep_lo, keep_hi = neighbours(a, first, last)
        for t in range(TILES):
            x = jnp.concatenate(
                [sr[lo, 0, t].astype(F32) * keep_lo, sr[a, 1, t].astype(F32), sr[hi, 2, t].astype(F32) * keep_hi], axis=0
            )
            a_rows[a, :, 128 * t : 128 * t + 128] = x.astype(BF16)
        return 0

    lax.fori_loop(0, NA, spread, 0, unroll=2)
    half = 64 * TILES
    left = a_rows[...].reshape(24 * NA, 128 * TILES)
    left = left[:, :half], left[:, half:]

    def times(x, y):
        return lax.dot_general(x, y, (((1,), (1,)), ((), ())), preferred_element_type=F32)

    for n in range(NZ + 1):
        right = b_rows[n, :, :half], b_rows[n, :, half:]
        value = times(left[0], right[0]) - times(left[1], right[1])
        pred[0, :, :, 128 * n : 128 * n + 128] = value.reshape(NA, 24, 128)
        value = times(left[0], right[1]) + times(left[1], right[0])
        pred[1, :, :, 128 * n : 128 * n + 128] = value.reshape(NA, 24, 128)

    def data_of(a):
        lo, hi, keep_lo, keep_hi = neighbours(a, first, last)
        data = []
        for part in range(2):
            below, _ = sides(core, rec_partner[part, lo].astype(F32), rec_beyond[part, lo].astype(F32))
            _, above = sides(core, rec_partner[part, hi].astype(F32), rec_beyond[part, hi].astype(F32))
            data.append(jnp.concatenate([below * keep_lo, rec[part, a].astype(F32), above * keep_hi], axis=0))
        return data

    def terms_of(dr, di, pr, pi):
        return pr * dr + pi * di, pr * di - pi * dr, pr * pr + pi * pi

    def subtract(dr, di, pr, pi, sums):
        den = sums[2] + EPS
        gain_re, gain_im = sums[0] / den, sums[1] / den
        return dr - (gain_re * pr - gain_im * pi), di - (gain_re * pi + gain_im * pr)

    def first_sweep(a, _):
        dr, di = data_of(a)
        guess = []
        for part in range(2):
            full = pred[part, a]
            mult[part, a] = (full[8:16, :512] * (768.0 ** -0.5)).astype(BF16)
            full = full.astype(BF16).astype(F32)
            pred[part, a] = full
            guess.append(full)
        weight = 1.5 - jnp.tanh(dr * dr + di * di)
        for n, q in enumerate(terms_of(dr, di, *guess)):
            once[n, a] = windows_rows(weight * q, 16)
        return 0

    lax.fori_loop(0, NA, first_sweep, 0, unroll=2)
    far = lax.broadcasted_iota(jnp.int32, (512, 256), 0) - lax.broadcasted_iota(jnp.int32, (512, 256), 1) - 128
    band = (jnp.abs(far) <= REACH).astype(F32).astype(BF16)
    windows_lanes(once, box, band, (0, 2, 4))

    def second_sweep(a, _):
        dr, di = [v[4:20] for v in data_of(a)]
        pr, pi = pred[0, a, 4:20], pred[1, a, 4:20]
        er, ei = subtract(dr, di, pr, pi, [box[n, a] for n in range(3)])
        weight = 1.5 - jnp.tanh(er * er + ei * ei)
        for n, q in enumerate(terms_of(dr, di, pr, pi)):
            once[n, a, :8] = windows_rows(weight * q, 8)
        return 0

    lax.fori_loop(0, NA, second_sweep, 0, unroll=2)
    windows_lanes(once.at[:, :, :8], box.at[:, :, :8], band, (0, 2))

    def finish(a, _):
        dr, di = rec[0, a, :, :512].astype(F32), rec[1, a, :, :512].astype(F32)
        pr, pi = pred[0, a, 8:16, :512], pred[1, a, 8:16, :512]
        er, ei = subtract(dr, di, pr, pi, [box[n, a, :8, :512] for n in range(3)])
        prim[0, a], prim[1, a] = er.astype(BF16), ei.astype(BF16)
        return 0

    lax.fori_loop(0, NA, finish, 0, unroll=2)


def shape(*dims):
    return jax.ShapeDtypeStruct(dims, BF16)


def ring(count, step, closed):
    return [(n, (n + step) % count) for n in range(count) if closed or 0 <= n + step < count]


def block(record, panel_offset):
    src_count, rcv_count = lax.axis_size("src"), lax.axis_size("rcv")
    src, rcv = lax.axis_index("src"), lax.axis_index("rcv")
    pos = jnp.stack([src, rcv]).astype(jnp.int32)
    rec = record[0]
    plane = [[z * NP + p for p in range(NP)] for z in range(NZ)]
    column = [[z * NP + p for z in range(NZ)] for p in range(NP)]
    line = [[z * NP + y * NC + c for y in range(NY)] for z in range(NZ) for c in range(NC)]
    swap = [(n, n ^ 1) for n in range(rcv_count)]
    beyond = [(n, (n + (1 if n % 2 else -1)) % rcv_count) for n in range(rcv_count)]

    def exchange(x, axis, groups=None):
        return lax.all_to_all(x, axis, split_axis=0, concat_axis=0, tiled=True, axis_index_groups=groups)

    def copies(x, count, axis, groups=None):
        return exchange(jnp.broadcast_to(x, (count, *x.shape)), axis, groups)

    def kernel(body, outs, scalars, arrays, scratch=(), flops=1 << 20, moved=1 << 20):
        return pl.pallas_call(
            body,
            out_shape=outs,
            in_specs=smem(len(scalars)) + vmem(len(arrays)),
            out_specs=jax.tree.map(lambda _: vmem(1)[0], outs),
            scratch_shapes=scratch,
            cost_estimate=pl.CostEstimate(flops=flops, bytes_accessed=moved, transcendentals=0),
        )(*scalars, *arrays)

    to_src = kernel(pick_behind_kernel, shape(NA, 8, 128), (pos, panel_offset), (rec,))
    from_src = exchange(to_src, "src")
    to_rcv = kernel(pick_front_kernel, shape(NP, 8, 128), (pos, panel_offset), (rec,))
    from_rcv = exchange(to_rcv, "rcv", plane)
    behind = kernel(order_behind_kernel, shape(TILES, 8, 128), (), (from_src,))
    message = kernel(order_kernel, shape(NZ, 2 * TILES, 8, 128), (pos,), (from_rcv, behind))
    pieces = exchange(message, "rcv", column)
    held, _ = lax.optimization_barrier((rec, from_rcv))
    first_tile, last_tile = held[:, :, :128], held[:, :, 384:]
    next_src = lax.ppermute(first_tile, "src", ring(src_count, -1, False))
    last_src = lax.ppermute(last_tile, "src", ring(src_count, 1, False))
    lane = lax.broadcasted_iota(jnp.int32, (1, 1, 128), 2)
    rim = jnp.where(lane < 8, next_src, jnp.where(lane >= 120, last_src, jnp.zeros_like(last_src)))
    wide = jnp.concatenate([rec, rim], axis=2).reshape(2, NA, 8, EXT)
    pieces, wide = lax.optimization_barrier((pieces, wide))
    rows, own = kernel(average_kernel, (shape(NZ, TILES, 8, 128), shape(TILES, 8, 128)), (pos,), (pieces,))
    ss = copies(rows, NY, "rcv", line)
    near = own
    own_partner = lax.ppermute(near, "rcv", swap)
    own_beyond = lax.ppermute(near, "rcv", beyond)
    wide_partner = lax.ppermute(wide, "rcv", swap)
    wide_beyond = lax.ppermute(wide, "rcv", beyond)
    even_core = rcv % 2 == 0
    own = jnp.stack(
        [jnp.where(even_core, own_beyond, own_partner), own, jnp.where(even_core, own_partner, own_beyond)]
    )
    ss, own, wide_partner, wide_beyond = lax.optimization_barrier((ss, own, wide_partner, wide_beyond))
    sr = copies(own, src_count, "src")
    sp = lax.ppermute(ss, "rcv", swap)
    row_first = jnp.where(even_core, ss[0, 0], sp[0, 0])
    row_last = jnp.where(even_core, sp[NY - 1, NZ - 1], ss[NY - 1, NZ - 1])
    row_hi = lax.ppermute(row_first, "src", ring(src_count, -1, False))
    row_lo = lax.ppermute(row_last, "src", ring(src_count, 1, False))
    prim, mult = kernel(
        final_kernel,
        (shape(2, NA, 8, 512),) * 2,
        (pos,),
        (wide, wide_partner, wide_beyond, sr, ss, sp, row_hi, row_lo),
        [
            pltpu.VMEM((NA, 24, 128 * TILES), BF16),
            pltpu.VMEM((NZ + 1, 128, 128 * TILES), BF16),
            pltpu.VMEM((2, NA, 24, EXT), F32),
            pltpu.VMEM((3, NA, 16, EXT), F32),
            pltpu.VMEM((3, NA, 16, EXT), F32),
        ],
    )
    return prim.reshape(record.shape), mult.reshape(record.shape)


def solution(mesh):
    in_specs = (P(None, None, "rcv", "src"), P())
    out_specs = (P(None, None, "rcv", "src"), P(None, None, "rcv", "src"))
    return jax.shard_map(block, mesh=mesh, in_specs=in_specs, out_specs=out_specs, check_vma=False)
```

```python
import jax
import jax.numpy as jnp
from jax import lax
from jax.experimental import pallas as pl
from jax.experimental.pallas import tpu as pltpu
from jax.sharding import PartitionSpec as P

NZ, NY, NC = 4, 8, 2
NP = NY * NC
NA = 12
TILES = 3 * NZ
EXT = 640
STRIDE = 8
REACH = 4
EPS = 1e-6
F32, BF16 = jnp.float32, jnp.bfloat16


def vmem(count):
    return [pl.BlockSpec(memory_space=pltpu.VMEM)] * count


def smem(count):
    return [pl.BlockSpec(memory_space=pltpu.SMEM)] * count


def position():
    return lax.axis_index("src"), lax.axis_index("rcv")


def replicate(source, target, sems):
    copies = [pltpu.make_async_copy(source, target.at[n], sems.at[n]) for n in range(target.shape[0])]
    for copy in copies:
        copy.start()
    for copy in copies:
        copy.wait()


def pick_behind_kernel(panel, rec, to_src):
    pos = position()
    lane = lax.broadcasted_iota(jnp.int32, (1, 128), 1)
    early = pos[0] < 8
    key_part = jnp.where(early, lane % 8 // 4, lane // 64)
    key_pos = 16 * (lane % 4) + jnp.where(early, lane // 8, lane % 64 // 4)
    offset = jnp.zeros((1, 128), jnp.int32)
    for g in range(64):
        offset = jnp.where(key_pos == g, panel[64 * pos[0] + g], offset)
    key_row = STRIDE * key_pos + offset
    rows = lax.broadcasted_iota(jnp.int32, (512, 128), 0)
    total = jnp.zeros((96, 128), F32)
    for part in range(2):
        chosen = ((rows == key_row) & (key_part == part)).astype(F32).astype(BF16)
        total += jnp.dot(rec[part], chosen, preferred_element_type=F32)
    to_src[...] = total.astype(BF16).reshape(NA, 8, 128)


def pick_front_kernel(panel, rec, to_rcv):
    pos = position()
    lane = lax.broadcasted_iota(jnp.int32, (1, 128), 1)
    kind, slot, run_z = lane % 32 // 8, lane % 8, lane // 32
    run = jnp.where(kind < 2, slot, jnp.where(kind == 2, 8 + slot % 4, NA))
    run_part = jnp.where(kind < 2, kind, slot // 4)
    offset = jnp.zeros((1, 128), jnp.int32)
    for a in range(NA):
        offset = jnp.where(run == a, panel[64 * a + pos[1]], offset)
    col = jnp.where(run < NA, STRIDE * run + offset, -1)
    rows = lax.broadcasted_iota(jnp.int32, (96, 128), 0)
    total = jnp.zeros((128, 128), F32)
    for z in range(NZ):
        for part in range(2):
            chosen = ((rows == col) & (run_part == part) & (run_z == z)).astype(F32).astype(BF16)
            total += lax.dot_general(
                rec[part, :, 128 * z : 128 * z + 128],
                chosen,
                (((0,), (0,)), ((), ())),
                preferred_element_type=F32,
            )
    to_rcv[...] = total.astype(BF16).reshape(NP, 8, 128)


def turned(x, shift):
    return pltpu.roll(x, shift % 128, 1) if shift % 128 else x


def order_behind_kernel(from_src, behind):
    lane = lax.broadcasted_iota(jnp.int32, (8, 128), 1)
    tiles = [from_src[a].astype(F32) for a in range(NA)]
    for part in range(2):
        for pair in range(2):
            for kind in range(2):
                acc = jnp.zeros((8, 128), F32)
                for a in range(8):
                    acc = jnp.where(lane % 8 == a, turned(tiles[a], a - (4 * part + 2 * pair + kind)), acc)
                behind[6 * part + 3 * pair + kind] = acc.astype(BF16)
            acc = jnp.zeros((8, 128), F32)
            for odd in range(2):
                for a in range(8, NA):
                    shift = 64 * (odd - part) + a - 8 - (2 * pair + odd)
                    acc = jnp.where((lane // 64 == odd) & (lane % 4 == a - 8), turned(tiles[a], shift), acc)
            behind[6 * part + 3 * pair + 2] = acc.astype(BF16)


def order_kernel(from_rcv, behind, out):
    pos = position()
    lane = lax.broadcasted_iota(jnp.int32, (8, 128), 1)
    tiles = [from_rcv[p].astype(F32) for p in range(NP)]
    odd = pos[1] // NP % 2 == 1
    for z in range(NZ):
        for kind in range(3):
            acc = jnp.zeros((8, 128), F32)
            for p in range(NP):
                if kind < 2:
                    acc = jnp.where(lane // 8 == p, turned(tiles[p], 8 * p - 32 * z - 8 * kind), acc)
                else:
                    for part in range(2):
                        shift = 64 * part + 4 * p - 32 * z - 16 - 4 * part
                        acc = jnp.where(lane // 4 == 16 * part + p, turned(tiles[p], shift), acc)
            if kind == 2:
                acc = jnp.where(odd, pltpu.roll(acc, 64, 1), acc)
            tile = acc.astype(BF16)
            for copy in range(NZ):
                out[copy, 3 * z + kind] = tile
    for copy in range(NZ):
        out[copy, TILES:] = behind[...]


def average_kernel(pieces, rec, next_src, last_src, out, near, rows, sems):
    lane = lax.broadcasted_iota(jnp.int32, (8, 128), 1)
    low = lane < 64
    for z in range(NZ):
        for tile in range(TILES):
            part, pair, kind = tile // 6, tile % 6 // 3, tile % 3
            if kind < 2:
                front = pieces[2 * pair + kind, 3 * z + part].astype(F32)
            else:
                even, odd = [pieces[2 * pair + n, 3 * z + 2].astype(F32) for n in range(2)]
                front = pltpu.roll(jnp.where(low, odd, even), 64, 1) if part else jnp.where(low, even, odd)
            rows[z, tile] = ((front + pieces[z, TILES + tile].astype(F32)) * 0.5).astype(BF16)
    copies = [pltpu.make_async_copy(rows, out.at[n], sems.at[n]) for n in range(NY)]
    for copy in copies:
        copy.start()
    near[:TILES] = rows[position()[1] // NP]
    for part in range(2):
        for a in range(NA):
            first = TILES + (part * NA + a) * (EXT // 128)
            run = slice(8 * a, 8 * a + 8)
            for n in range(EXT // 128 - 1):
                near[first + n] = rec[part, run, 128 * n : 128 * n + 128]
            after, before = next_src[part, run].astype(F32), last_src[part, run].astype(F32)
            rim = jnp.where(lane < 8, after, jnp.where(lane >= 120, before, jnp.zeros_like(before)))
            near[first + EXT // 128 - 1] = rim.astype(BF16)
    for copy in copies:
        copy.wait()


def stack_kernel(near, partner, beyond, out, rows, sems):
    core = position()[1] % 2
    for t in range(TILES):
        one, two = partner[t].astype(F32), beyond[t].astype(F32)
        rows[0, t] = jnp.where(core == 0, two, one).astype(BF16)
        rows[1, t] = near[t]
        rows[2, t] = jnp.where(core == 0, one, two).astype(BF16)
    replicate(rows, out, sems)


def bounds(rcv):
    return (rcv == 0).astype(jnp.int32), (rcv == NZ * NP - 1).astype(jnp.int32)


def sides(core, partner, beyond):
    return jnp.where(core == 0, beyond, partner), jnp.where(core == 0, partner, beyond)


def neighbours(a, first, last):
    keep_lo = (a - first >= 0).astype(F32)
    keep_hi = (a + last <= NA - 1).astype(F32)
    return jnp.maximum(a - first, 0), jnp.minimum(a + last, NA - 1), keep_lo, keep_hi


def windows_rows(x, count):
    two = x[:-1] + x[1:]
    four = two[:-2] + two[2:]
    eight = four[:-4] + four[4:]
    return eight[:count] + x[8 : 8 + count]


def windows_lanes(source, target, band, pairs):
    count = EXT // 128
    rows = source.shape[0] * source.shape[1] * source.shape[2]
    tiles = []
    for n in range(count):
        x = source[:, :, :, 128 * n : 128 * n + 128].reshape(rows, 128)
        high = x.astype(BF16)
        tiles.append((high, (x - high.astype(F32)).astype(BF16)))
    for n in pairs:
        width = min(2, count - n)
        total = jnp.zeros((rows, 128 * width), F32)
        for half in range(2):
            near = jnp.concatenate([tiles[(n + m) % count][half] for m in range(-1, width + 1)], axis=1)
            total += jnp.dot(near, band[: 128 * (width + 2), : 128 * width], preferred_element_type=F32)
        target[:, :, :, 128 * n : 128 * (n + width)] = total.reshape(*target.shape[:3], 128 * width)


def spread_rows(sr, a_rows, first, last):
    def spread(a, _):
        lo, hi, keep_lo, keep_hi = neighbours(a, first, last)
        for t in range(TILES):
            x = jnp.concatenate(
                [sr[lo, 0, t].astype(F32) * keep_lo, sr[a, 1, t].astype(F32), sr[hi, 2, t].astype(F32) * keep_hi], axis=0
            )
            a_rows[a, :, 128 * t : 128 * t + 128] = x.astype(BF16)
        return 0

    lax.fori_loop(0, NA, spread, 0, unroll=2)
    left = a_rows[...].reshape(24 * NA, 128 * TILES)
    return left[:, : 64 * TILES], left[:, 64 * TILES :]


def times(x, y):
    return lax.dot_general(x, y, (((1,), (1,)), ((), ())), preferred_element_type=F32)


def predict_kernel(sr, ss, sp, guess, mult, a_rows, b_rows):
    rcv = position()[1]
    core = rcv % 2
    left = spread_rows(sr, a_rows, *bounds(rcv))
    for z in range(NZ):
        for t in range(TILES):
            mine, theirs = ss[:, z, t].astype(F32), sp[:, z, t].astype(F32)
            zero = jnp.where(core == 0, mine, theirs)
            one = jnp.where(core == 0, theirs, mine)
            x = jnp.stack([zero, one], axis=1).reshape(128, 128)
            b_rows[128 * z : 128 * z + 128, 128 * t : 128 * t + 128] = x.astype(BF16)
    for n in range(NZ // 2):
        cols = slice(256 * n, 256 * n + 256)
        right = b_rows[cols, : 64 * TILES], b_rows[cols, 64 * TILES :]
        value = (
            times(left[0], right[0]) - times(left[1], right[1]),
            times(left[0], right[1]) + times(left[1], right[0]),
        )
        for part in range(2):
            full = value[part].reshape(NA, 24, 256)
            guess[part, :, :, cols] = full.astype(BF16)
            mult[part, :, :, cols] = (full[:, 8:16] * (768.0 ** -0.5)).astype(BF16)


def subtract_kernel(near, near_partner, near_beyond, guess, sr, row_hi, row_lo, prim, a_rows, edge, once, box):
    rcv = position()[1]
    core = rcv % 2
    first, last = bounds(rcv)
    left = spread_rows(sr, a_rows, first, last)
    right = []
    for part in range(2):
        tiles = range(6 * part, 6 * part + 6)
        right.append(
            jnp.concatenate(
                [
                    jnp.concatenate([row_hi[t].astype(F32) for t in tiles], axis=1),
                    jnp.zeros((112, 64 * TILES), F32),
                    jnp.concatenate([row_lo[t].astype(F32) for t in tiles], axis=1),
                ],
                axis=0,
            ).astype(BF16)
        )
    straight = times(left[0], jnp.concatenate(right, axis=0))
    crossed = times(left[1], jnp.concatenate(right[::-1], axis=0))
    edge[0] = (straight[:, :128] - crossed[:, :128]).astype(BF16).astype(F32).reshape(NA, 24, 128)
    edge[1] = (straight[:, 128:] + crossed[:, 128:]).astype(BF16).astype(F32).reshape(NA, 24, 128)

    def run_of(ref, part, a):
        start = TILES + (part * NA + a) * (EXT // 128)
        return jnp.concatenate([ref[start + n].astype(F32) for n in range(EXT // 128)], axis=1)

    def data_of(a):
        lo, hi, keep_lo, keep_hi = neighbours(a, first, last)
        data = []
        for part in range(2):
            below, _ = sides(core, run_of(near_partner, part, lo), run_of(near_beyond, part, lo))
            _, above = sides(core, run_of(near_partner, part, hi), run_of(near_beyond, part, hi))
            data.append(jnp.concatenate([below * keep_lo, run_of(near, part, a), above * keep_hi], axis=0))
        return data

    def guess_of(a):
        return [jnp.concatenate([guess[part, a].astype(F32), edge[part, a]], axis=1) for part in range(2)]

    def terms_of(dr, di, pr, pi):
        return pr * dr + pi * di, pr * di - pi * dr, pr * pr + pi * pi

    def subtract(dr, di, pr, pi, sums):
        den = sums[2] + EPS
        gain_re, gain_im = sums[0] / den, sums[1] / den
        return dr - (gain_re * pr - gain_im * pi), di - (gain_re * pi + gain_im * pr)

    def first_sweep(a, _):
        dr, di = data_of(a)
        weight = 1.5 - jnp.tanh(dr * dr + di * di)
        for n, q in enumerate(terms_of(dr, di, *guess_of(a))):
            once[n, a] = windows_rows(weight * q, 16)
        return 0

    lax.fori_loop(0, NA, first_sweep, 0, unroll=2)
    far = lax.broadcasted_iota(jnp.int32, (512, 256), 0) - lax.broadcasted_iota(jnp.int32, (512, 256), 1) - 128
    band = (jnp.abs(far) <= REACH).astype(F32).astype(BF16)
    windows_lanes(once, box, band, (0, 2, 4))

    def second_sweep(a, _):
        dr, di, pr, pi = [v[4:20] for v in (*data_of(a), *guess_of(a))]
        er, ei = subtract(dr, di, pr, pi, [box[n, a] for n in range(3)])
        weight = 1.5 - jnp.tanh(er * er + ei * ei)
        for n, q in enumerate(terms_of(dr, di, pr, pi)):
            once[n, a, :8] = windows_rows(weight * q, 8)
        return 0

    lax.fori_loop(0, NA, second_sweep, 0, unroll=2)
    windows_lanes(once.at[:, :, :8], box.at[:, :, :8], band, (0, 2))

    def finish(a, _):
        dr, di = [run_of(near, part, a)[:, :512] for part in range(2)]
        pr, pi = [guess[part, a].astype(F32)[8:16] for part in range(2)]
        er, ei = subtract(dr, di, pr, pi, [box[n, a, :8, :512] for n in range(3)])
        prim[0, a], prim[1, a] = er.astype(BF16), ei.astype(BF16)
        return 0

    lax.fori_loop(0, NA, finish, 0, unroll=2)


def shape(*dims):
    return jax.ShapeDtypeStruct(dims, BF16)


def ring(count, step, closed):
    return [(n, (n + step) % count) for n in range(count) if closed or 0 <= n + step < count]


def block(record, panel_offset):
    src_count, rcv_count = lax.axis_size("src"), lax.axis_size("rcv")
    rcv = lax.axis_index("rcv")
    rec = record[0]
    plane = [[z * NP + p for p in range(NP)] for z in range(NZ)]
    column = [[z * NP + p for z in range(NZ)] for p in range(NP)]
    line = [[z * NP + y * NC + c for y in range(NY)] for z in range(NZ) for c in range(NC)]
    swap = [(n, n ^ 1) for n in range(rcv_count)]
    beyond = [(n, (n + (1 if n % 2 else -1)) % rcv_count) for n in range(rcv_count)]

    def exchange(x, axis, groups=None):
        return lax.all_to_all(x, axis, split_axis=0, concat_axis=0, tiled=True, axis_index_groups=groups)

    def kernel(body, outs, scalars, arrays, scratch=(), flops=1 << 20, limit=8 << 20, spaces=None):
        spaces = spaces or jax.tree.map(lambda _: pltpu.VMEM, outs)
        return pl.pallas_call(
            body,
            out_shape=outs,
            in_specs=smem(len(scalars)) + vmem(len(arrays)),
            out_specs=jax.tree.map(lambda m: pl.BlockSpec(memory_space=m), spaces),
            scratch_shapes=scratch,
            compiler_params=pltpu.CompilerParams(vmem_limit_bytes=limit),
            cost_estimate=pl.CostEstimate(flops=flops, bytes_accessed=1 << 20, transcendentals=0),
        )(*scalars, *arrays)

    to_src = kernel(pick_behind_kernel, shape(NA, 8, 128), (panel_offset,), (rec,))
    from_src = exchange(to_src, "src")
    to_rcv = kernel(pick_front_kernel, shape(NP, 8, 128), (panel_offset,), (rec,))
    from_rcv = exchange(to_rcv, "rcv", plane)
    behind = kernel(order_behind_kernel, shape(TILES, 8, 128), (), (from_src,))
    message = kernel(order_kernel, shape(NZ, 2 * TILES, 8, 128), (), (from_rcv, behind))
    pieces = exchange(message, "rcv", column)
    held, _ = lax.optimization_barrier((rec, from_rcv))
    first_tile, last_tile = held[:, :, :128], held[:, :, 384:]
    next_src = lax.ppermute(first_tile, "src", ring(src_count, -1, False))
    last_src = lax.ppermute(last_tile, "src", ring(src_count, 1, False))
    spread, near = kernel(
        average_kernel,
        (shape(NY, NZ, TILES, 8, 128), shape(TILES + 2 * NA * (EXT // 128), 8, 128)),
        (),
        (pieces, rec, next_src, last_src),
        [pltpu.VMEM((NZ, TILES, 8, 128), BF16), pltpu.SemaphoreType.DMA((NY,))],
        spaces=(pltpu.HBM, pltpu.VMEM),
    )
    ss = exchange(spread, "rcv", line)
    near_partner = lax.ppermute(near, "rcv", swap)
    near_beyond = lax.ppermute(near, "rcv", beyond)
    stacked = kernel(
        stack_kernel,
        shape(src_count, 3, TILES, 8, 128),
        (),
        (near, near_partner, near_beyond),
        [pltpu.VMEM((3, TILES, 8, 128), BF16), pltpu.SemaphoreType.DMA((src_count,))],
        spaces=pltpu.HBM,
    )
    ss, stacked = lax.optimization_barrier((ss, stacked))
    sr = exchange(stacked, "src")
    sp = lax.ppermute(ss, "rcv", swap)
    even_core = rcv % 2 == 0
    row_first = jnp.where(even_core, ss[0, 0], sp[0, 0])
    row_last = jnp.where(even_core, sp[NY - 1, NZ - 1], ss[NY - 1, NZ - 1])
    row_hi = lax.ppermute(row_first, "src", ring(src_count, -1, False))
    row_lo = lax.ppermute(row_last, "src", ring(src_count, 1, False))
    guess, mult = kernel(
        predict_kernel,
        (shape(2, NA, 24, 512), shape(2, NA, 8, 512)),
        (),
        (sr, ss, sp),
        [pltpu.VMEM((NA, 24, 128 * TILES), BF16), pltpu.VMEM((512, 128 * TILES), BF16)],
        flops=1 << 32,
        limit=16 << 20,
    )
    prim = kernel(
        subtract_kernel,
        shape(2, NA, 8, 512),
        (),
        (near, near_partner, near_beyond, guess, sr, row_hi, row_lo),
        [
            pltpu.VMEM((NA, 24, 128 * TILES), BF16),
            pltpu.VMEM((2, NA, 24, 128), F32),
            pltpu.VMEM((3, NA, 16, EXT), F32),
            pltpu.VMEM((3, NA, 16, EXT), F32),
        ],
        flops=1 << 32,
        limit=20 << 20,
    )
    return prim.reshape(record.shape), mult.reshape(record.shape)


def solution(mesh):
    in_specs = (P(None, None, "rcv", "src"), P())
    out_specs = (P(None, None, "rcv", "src"), P(None, None, "rcv", "src"))
    return jax.shard_map(block, mesh=mesh, in_specs=in_specs, out_specs=out_specs, check_vma=False)
```

```python
import jax
import jax.numpy as jnp
from jax import lax
from jax.experimental import pallas as pl
from jax.experimental.pallas import tpu as pltpu
from jax.sharding import PartitionSpec as P

NZ, NY, NC = 4, 8, 2
NP = NY * NC
NA = 12
TILES = 3 * NZ
EXT = 640
STRIDE = 8
REACH = 4
EPS = 1e-6
F32, BF16 = jnp.float32, jnp.bfloat16


def vmem(count):
    return [pl.BlockSpec(memory_space=pltpu.VMEM)] * count


def smem(count):
    return [pl.BlockSpec(memory_space=pltpu.SMEM)] * count


def position():
    return lax.axis_index("src"), lax.axis_index("rcv")


def pick_behind_kernel(panel, rec, to_src):
    pos = position()
    lane = lax.broadcasted_iota(jnp.int32, (1, 128), 1)
    early = pos[0] < 8
    key_part = jnp.where(early, lane % 8 // 4, lane // 64)
    key_pos = 16 * (lane % 4) + jnp.where(early, lane // 8, lane % 64 // 4)
    offset = jnp.zeros((1, 128), jnp.int32)
    for g in range(64):
        offset = jnp.where(key_pos == g, panel[64 * pos[0] + g], offset)
    key_row = STRIDE * key_pos + offset
    rows = lax.broadcasted_iota(jnp.int32, (512, 128), 0)
    total = jnp.zeros((96, 128), F32)
    for part in range(2):
        chosen = ((rows == key_row) & (key_part == part)).astype(F32).astype(BF16)
        total += jnp.dot(rec[part], chosen, preferred_element_type=F32)
    to_src[...] = total.astype(BF16).reshape(NA, 8, 128)


def pick_front_kernel(panel, rec, to_rcv):
    pos = position()
    lane = lax.broadcasted_iota(jnp.int32, (1, 128), 1)
    kind, slot, run_z = lane % 32 // 8, lane % 8, lane // 32
    run = jnp.where(kind < 2, slot, jnp.where(kind == 2, 8 + slot % 4, NA))
    run_part = jnp.where(kind < 2, kind, slot // 4)
    offset = jnp.zeros((1, 128), jnp.int32)
    for a in range(NA):
        offset = jnp.where(run == a, panel[64 * a + pos[1]], offset)
    col = jnp.where(run < NA, STRIDE * run + offset, -1)
    rows = lax.broadcasted_iota(jnp.int32, (96, 128), 0)
    total = jnp.zeros((128, 128), F32)
    for z in range(NZ):
        for part in range(2):
            chosen = ((rows == col) & (run_part == part) & (run_z == z)).astype(F32).astype(BF16)
            total += lax.dot_general(
                rec[part, :, 128 * z : 128 * z + 128],
                chosen,
                (((0,), (0,)), ((), ())),
                preferred_element_type=F32,
            )
    to_rcv[...] = total.astype(BF16).reshape(NP, 8, 128)


def turned(x, shift):
    return pltpu.roll(x, shift % 128, 1) if shift % 128 else x


def order_behind_kernel(from_src, behind):
    lane = lax.broadcasted_iota(jnp.int32, (8, 128), 1)
    tiles = [from_src[a].astype(F32) for a in range(NA)]
    for part in range(2):
        for pair in range(2):
            for kind in range(2):
                acc = jnp.zeros((8, 128), F32)
                for a in range(8):
                    acc = jnp.where(lane % 8 == a, turned(tiles[a], a - (4 * part + 2 * pair + kind)), acc)
                behind[6 * part + 3 * pair + kind] = acc.astype(BF16)
            acc = jnp.zeros((8, 128), F32)
            for odd in range(2):
                for a in range(8, NA):
                    shift = 64 * (odd - part) + a - 8 - (2 * pair + odd)
                    acc = jnp.where((lane // 64 == odd) & (lane % 4 == a - 8), turned(tiles[a], shift), acc)
            behind[6 * part + 3 * pair + 2] = acc.astype(BF16)


def order_kernel(from_rcv, behind, out):
    pos = position()
    lane = lax.broadcasted_iota(jnp.int32, (8, 128), 1)
    tiles = [from_rcv[p].astype(F32) for p in range(NP)]
    odd = pos[1] // NP % 2 == 1
    for z in range(NZ):
        for kind in range(3):
            acc = jnp.zeros((8, 128), F32)
            for p in range(NP):
                if kind < 2:
                    acc = jnp.where(lane // 8 == p, turned(tiles[p], 8 * p - 32 * z - 8 * kind), acc)
                else:
                    for part in range(2):
                        shift = 64 * part + 4 * p - 32 * z - 16 - 4 * part
                        acc = jnp.where(lane // 4 == 16 * part + p, turned(tiles[p], shift), acc)
            if kind == 2:
                acc = jnp.where(odd, pltpu.roll(acc, 64, 1), acc)
            tile = acc.astype(BF16)
            for copy in range(NZ):
                out[copy, 3 * z + kind] = tile
    for copy in range(NZ):
        out[copy, TILES:] = behind[...]


def average_kernel(pieces, out, own, rows, sems):
    low = lax.broadcasted_iota(jnp.int32, (8, 128), 1) < 64
    for z in range(NZ):
        for tile in range(TILES):
            part, pair, kind = tile // 6, tile % 6 // 3, tile % 3
            if kind < 2:
                front = pieces[2 * pair + kind, 3 * z + part].astype(F32)
            else:
                even, odd = [pieces[2 * pair + n, 3 * z + 2].astype(F32) for n in range(2)]
                front = pltpu.roll(jnp.where(low, odd, even), 64, 1) if part else jnp.where(low, even, odd)
            rows[z, tile] = ((front + pieces[z, TILES + tile].astype(F32)) * 0.5).astype(BF16)
    copies = [pltpu.make_async_copy(rows, out.at[n], sems.at[n]) for n in range(NY)]
    for copy in copies:
        copy.start()
    own[...] = rows[position()[1] // NP]
    for copy in copies:
        copy.wait()


def widen_kernel(rec, next_src, last_src, wide):
    lane = lax.broadcasted_iota(jnp.int32, (8, 128), 1)
    for part in range(2):
        for a in range(NA):
            run = slice(8 * a, 8 * a + 8)
            for n in range(EXT // 128 - 1):
                wide[part, a, n] = rec[part, run, 128 * n : 128 * n + 128]
            after, before = next_src[part, run].astype(F32), last_src[part, run].astype(F32)
            rim = jnp.where(lane < 8, after, jnp.where(lane >= 120, before, jnp.zeros_like(before)))
            wide[part, a, EXT // 128 - 1] = rim.astype(BF16)


def bounds(rcv):
    return (rcv == 0).astype(jnp.int32), (rcv == NZ * NP - 1).astype(jnp.int32)


def sides(core, partner, beyond):
    return jnp.where(core == 0, beyond, partner), jnp.where(core == 0, partner, beyond)


def neighbours(a, first, last):
    keep_lo = (a - first >= 0).astype(F32)
    keep_hi = (a + last <= NA - 1).astype(F32)
    return jnp.maximum(a - first, 0), jnp.minimum(a + last, NA - 1), keep_lo, keep_hi


def windows_rows(x, count):
    two = x[:-1] + x[1:]
    four = two[:-2] + two[2:]
    eight = four[:-4] + four[4:]
    return eight[:count] + x[8 : 8 + count]


def windows_lanes(source, target, band, pairs):
    count = EXT // 128
    rows = source.shape[0] * source.shape[1] * source.shape[2]
    tiles = []
    for n in range(count):
        x = source[:, :, :, 128 * n : 128 * n + 128].reshape(rows, 128)
        high = x.astype(BF16)
        tiles.append((high, (x - high.astype(F32)).astype(BF16)))
    for n in pairs:
        width = min(2, count - n)
        total = jnp.zeros((rows, 128 * width), F32)
        for half in range(2):
            near = jnp.concatenate([tiles[(n + m) % count][half] for m in range(-1, width + 1)], axis=1)
            total += jnp.dot(near, band[: 128 * (width + 2), : 128 * width], preferred_element_type=F32)
        target[:, :, :, 128 * n : 128 * (n + width)] = total.reshape(*target.shape[:3], 128 * width)


def spread_rows(sr, partner, beyond, a_rows):
    src, rcv = position()
    first, last = bounds(rcv)

    def held(a):
        return 4 * ((src + 3 - a % 3) % 3) + (src // 3 + 4 - a // 3) % 4

    def spread(a, _):
        lo, hi, keep_lo, keep_hi = neighbours(a, first, last)
        lo, hi, mid = held(lo), held(hi), held(a)
        for t in range(TILES):
            below, _ = sides(rcv % 2, partner[lo, t].astype(F32), beyond[lo, t].astype(F32))
            _, above = sides(rcv % 2, partner[hi, t].astype(F32), beyond[hi, t].astype(F32))
            x = jnp.concatenate([below * keep_lo, sr[mid, t].astype(F32), above * keep_hi], axis=0)
            a_rows[a, :, 128 * t : 128 * t + 128] = x.astype(BF16)
        return 0

    lax.fori_loop(0, NA, spread, 0, unroll=2)


def halves(a_rows):
    left = a_rows[...].reshape(24 * NA, 128 * TILES)
    return left[:, : 64 * TILES], left[:, 64 * TILES :]


def times(x, y):
    return lax.dot_general(x, y, (((1,), (1,)), ((), ())), preferred_element_type=F32)


def predict_kernel(sr, partner, beyond, ss, sp, guess, mult, a_rows, b_rows):
    core = position()[1] % 2
    spread_rows(sr, partner, beyond, a_rows)
    left = halves(a_rows)
    for z in range(NZ):
        for t in range(TILES):
            mine, theirs = ss[:, z, t].astype(F32), sp[:, z, t].astype(F32)
            zero = jnp.where(core == 0, mine, theirs)
            one = jnp.where(core == 0, theirs, mine)
            x = jnp.stack([zero, one], axis=1).reshape(128, 128)
            b_rows[128 * z : 128 * z + 128, 128 * t : 128 * t + 128] = x.astype(BF16)
    for n in range(NZ // 2):
        cols = slice(256 * n, 256 * n + 256)
        right = b_rows[cols, : 64 * TILES], b_rows[cols, 64 * TILES :]
        value = (
            times(left[0], right[0]) - times(left[1], right[1]),
            times(left[0], right[1]) + times(left[1], right[0]),
        )
        for part in range(2):
            full = value[part].reshape(NA, 24, 256)
            guess[part, :, :, cols] = full.astype(BF16)
            mult[part, :, :, cols] = (full[:, 8:16] * (768.0 ** -0.5)).astype(BF16)


def subtract_kernel(wide, partner, beyond, guess, a_rows, row_same, row_cross, prim, data, edge, once, box):
    rcv = position()[1]
    first, last = bounds(rcv)
    left = halves(a_rows)
    rims = [(row_same[t].astype(F32), row_cross[t].astype(F32)) for t in range(TILES)]
    row_hi = [jnp.where(rcv % 2 == 0, same, cross) for same, cross in rims]
    row_lo = [jnp.where(rcv % 2 == 0, cross, same) for same, cross in rims]
    right = []
    for part in range(2):
        tiles = range(6 * part, 6 * part + 6)
        right.append(
            jnp.concatenate(
                [
                    jnp.concatenate([row_hi[t] for t in tiles], axis=1),
                    jnp.zeros((112, 64 * TILES), F32),
                    jnp.concatenate([row_lo[t] for t in tiles], axis=1),
                ],
                axis=0,
            ).astype(BF16)
        )
    straight = times(left[0], jnp.concatenate(right, axis=0))
    crossed = times(left[1], jnp.concatenate(right[::-1], axis=0))
    edge[0] = (straight[:, :128] - crossed[:, :128]).astype(BF16).astype(F32).reshape(NA, 24, 128)
    edge[1] = (straight[:, 128:] + crossed[:, 128:]).astype(BF16).astype(F32).reshape(NA, 24, 128)

    def run_of(ref, part, a):
        return jnp.concatenate([ref[part, a, n].astype(F32) for n in range(EXT // 128)], axis=1)

    def guess_of(a):
        return [jnp.concatenate([guess[part, a].astype(F32), edge[part, a]], axis=1) for part in range(2)]

    def terms_of(dr, di, pr, pi):
        return pr * dr + pi * di, pr * di - pi * dr, pr * pr + pi * pi

    def subtract(dr, di, pr, pi, sums):
        den = sums[2] + EPS
        gain_re, gain_im = sums[0] / den, sums[1] / den
        return dr - (gain_re * pr - gain_im * pi), di - (gain_re * pi + gain_im * pr)

    def first_sweep(a, _):
        lo, hi, keep_lo, keep_hi = neighbours(a, first, last)
        for part in range(2):
            below, _ = sides(rcv % 2, run_of(partner, part, lo), run_of(beyond, part, lo))
            _, above = sides(rcv % 2, run_of(partner, part, hi), run_of(beyond, part, hi))
            data[part, a] = jnp.concatenate([below * keep_lo, run_of(wide, part, a), above * keep_hi], axis=0)
        dr, di = data[0, a], data[1, a]
        weight = 1.5 - jnp.tanh(dr * dr + di * di)
        for n, q in enumerate(terms_of(dr, di, *guess_of(a))):
            once[n, a] = windows_rows(weight * q, 16)
        return 0

    lax.fori_loop(0, NA, first_sweep, 0, unroll=2)
    far = lax.broadcasted_iota(jnp.int32, (512, 256), 0) - lax.broadcasted_iota(jnp.int32, (512, 256), 1) - 128
    band = (jnp.abs(far) <= REACH).astype(F32).astype(BF16)
    windows_lanes(once, box, band, (0, 2, 4))

    def second_sweep(a, _):
        dr, di = data[0, a, 4:20], data[1, a, 4:20]
        pr, pi = [v[4:20] for v in guess_of(a)]
        er, ei = subtract(dr, di, pr, pi, [box[n, a] for n in range(3)])
        again = 1.5 - jnp.tanh(er * er + ei * ei)
        for n, q in enumerate(terms_of(dr, di, pr, pi)):
            once[n, a, :8] = windows_rows(again * q, 8)
        return 0

    lax.fori_loop(0, NA, second_sweep, 0, unroll=2)
    windows_lanes(once.at[:, :, :8], box.at[:, :, :8], band, (0, 2))

    def finish(a, _):
        dr, di = [data[part, a, 8:16, :512] for part in range(2)]
        pr, pi = [guess[part, a].astype(F32)[8:16] for part in range(2)]
        er, ei = subtract(dr, di, pr, pi, [box[n, a, :8, :512] for n in range(3)])
        prim[0, a], prim[1, a] = er.astype(BF16), ei.astype(BF16)
        return 0

    lax.fori_loop(0, NA, finish, 0, unroll=2)


def shape(*dims):
    return jax.ShapeDtypeStruct(dims, BF16)


def ring(count, step, closed):
    return [(n, (n + step) % count) for n in range(count) if closed or 0 <= n + step < count]


def block(record, panel_offset):
    src_count, rcv_count = lax.axis_size("src"), lax.axis_size("rcv")
    rec = record[0]
    plane = [[z * NP + p for p in range(NP)] for z in range(NZ)]
    column = [[z * NP + p for z in range(NZ)] for p in range(NP)]
    line = [[z * NP + y * NC + c for y in range(NY)] for z in range(NZ) for c in range(NC)]
    swap = [(n, n ^ 1) for n in range(rcv_count)]
    beyond = [(n, (n + (1 if n % 2 else -1)) % rcv_count) for n in range(rcv_count)]

    def exchange(x, axis, groups=None):
        return lax.all_to_all(x, axis, split_axis=0, concat_axis=0, tiled=True, axis_index_groups=groups)

    def kernel(body, outs, scalars, arrays, scratch=(), flops=1 << 20, limit=8 << 20, spaces=None):
        spaces = spaces or jax.tree.map(lambda _: pltpu.VMEM, outs)
        return pl.pallas_call(
            body,
            out_shape=outs,
            in_specs=smem(len(scalars)) + vmem(len(arrays)),
            out_specs=jax.tree.map(lambda m: pl.BlockSpec(memory_space=m), spaces),
            scratch_shapes=scratch,
            compiler_params=pltpu.CompilerParams(vmem_limit_bytes=limit),
            cost_estimate=pl.CostEstimate(flops=flops, bytes_accessed=1 << 20, transcendentals=0),
        )(*scalars, *arrays)

    to_src = kernel(pick_behind_kernel, shape(NA, 8, 128), (panel_offset,), (rec,), limit=60 << 20)
    from_src = exchange(to_src, "src")
    to_rcv = kernel(pick_front_kernel, shape(NP, 8, 128), (panel_offset,), (rec,))
    from_rcv = exchange(to_rcv, "rcv", plane)
    behind = kernel(order_behind_kernel, shape(TILES, 8, 128), (), (from_src,))
    message = kernel(order_kernel, shape(NZ, 2 * TILES, 8, 128), (), (from_rcv, behind))
    pieces = exchange(message, "rcv", column)
    held, _ = lax.optimization_barrier((rec, from_src))
    first_tile, last_tile = held[:, :, :128], held[:, :, 384:]
    next_src = lax.ppermute(first_tile, "src", ring(src_count, -1, False))
    last_src = lax.ppermute(last_tile, "src", ring(src_count, 1, False))
    wide = kernel(widen_kernel, shape(2, NA, EXT // 128, 8, 128), (), (rec, next_src, last_src))
    wide_beyond = lax.ppermute(wide, "rcv", beyond)
    wide_partner = lax.ppermute(wide, "rcv", swap)
    spread, own = kernel(
        average_kernel,
        (shape(NY, NZ, TILES, 8, 128), shape(TILES, 8, 128)),
        (),
        (pieces,),
        [pltpu.VMEM((NZ, TILES, 8, 128), BF16), pltpu.SemaphoreType.DMA((NY,))],
        spaces=(pltpu.HBM, pltpu.VMEM),
    )
    ss = exchange(spread, "rcv", line)
    moved = [lax.ppermute(own, "src", ring(src_count, 3 * d, True)) for d in range(1, 4)]
    sr = jnp.stack([own, *moved])
    moved = [
        lax.ppermute(sr, "src", [(n, n - n % 3 + (n + e) % 3) for n in range(src_count)]) for e in range(1, 3)
    ]
    sr = jnp.concatenate([sr, *moved])
    sr_beyond = lax.ppermute(sr, "rcv", beyond)
    sr_partner = lax.ppermute(sr, "rcv", swap)
    row = jnp.where(lax.axis_index("rcv") % 2 == 0, ss[0, 0], ss[NY - 1, NZ - 1])
    same, cross = [
        [
            (n * rcv_count + k, to * rcv_count + (k ^ flip))
            for n in range(src_count)
            for k in range(rcv_count)
            for to in (n + (1 if k % 2 else -1),)
            if 0 <= to < src_count
        ]
        for flip in range(2)
    ]
    row_same = lax.ppermute(row, ("src", "rcv"), same)
    row_cross = lax.ppermute(row, ("src", "rcv"), cross)
    sp = lax.ppermute(ss, "rcv", swap)
    guess, mult, left = kernel(
        predict_kernel,
        (shape(2, NA, 24, 512), shape(2, NA, 8, 512), shape(NA, 24, 128 * TILES)),
        (),
        (sr, sr_partner, sr_beyond, ss, sp),
        [pltpu.VMEM((512, 128 * TILES), BF16)],
        flops=1 << 32,
        limit=16 << 20,
    )
    prim = kernel(
        subtract_kernel,
        shape(2, NA, 8, 512),
        (),
        (wide, wide_partner, wide_beyond, guess, left, row_same, row_cross),
        [
            pltpu.VMEM((2, NA, 24, EXT), F32),
            pltpu.VMEM((2, NA, 24, 128), F32),
            pltpu.VMEM((3, NA, 16, EXT), F32),
            pltpu.VMEM((3, NA, 16, EXT), F32),
        ],
        flops=1 << 32,
        limit=20 << 20,
    )
    return prim.reshape(record.shape), mult.reshape(record.shape)


def solution(mesh):
    in_specs = (P(None, None, "rcv", "src"), P())
    out_specs = (P(None, None, "rcv", "src"), P(None, None, "rcv", "src"))
    return jax.shard_map(block, mesh=mesh, in_specs=in_specs, out_specs=out_specs, check_vma=False)
```

```python
import jax
import jax.numpy as jnp
from jax import lax
from jax.experimental import pallas as pl
from jax.experimental.pallas import tpu as pltpu
from jax.sharding import PartitionSpec as P

NZ, NY, NC = 4, 8, 2
NP = NY * NC
NA = 12
TILES = 3 * NZ
EXT = 640
STRIDE = 8
REACH = 4
EPS = 1e-6
F32, BF16 = jnp.float32, jnp.bfloat16


def vmem(count):
    return [pl.BlockSpec(memory_space=pltpu.VMEM)] * count


def smem(count):
    return [pl.BlockSpec(memory_space=pltpu.SMEM)] * count


def position():
    return lax.axis_index("src"), lax.axis_index("rcv")


def pick_behind_kernel(panel, rec, to_src):
    pos = position()
    lane = lax.broadcasted_iota(jnp.int32, (1, 128), 1)
    early = pos[0] < 8
    key_part = jnp.where(early, lane % 8 // 4, lane // 64)
    key_pos = 16 * (lane % 4) + jnp.where(early, lane // 8, lane % 64 // 4)
    offset = jnp.zeros((1, 128), jnp.int32)
    for g in range(64):
        offset = jnp.where(key_pos == g, panel[64 * pos[0] + g], offset)
    key_row = STRIDE * key_pos + offset
    rows = lax.broadcasted_iota(jnp.int32, (512, 128), 0)
    total = jnp.zeros((96, 128), F32)
    for part in range(2):
        chosen = ((rows == key_row) & (key_part == part)).astype(F32).astype(BF16)
        total += jnp.dot(rec[part], chosen, preferred_element_type=F32)
    to_src[...] = total.astype(BF16).reshape(NA, 8, 128)


def pick_front_kernel(panel, rec, to_rcv):
    pos = position()
    lane = lax.broadcasted_iota(jnp.int32, (1, 128), 1)
    kind, slot, run_z = lane % 32 // 8, lane % 8, lane // 32
    run = jnp.where(kind < 2, slot, jnp.where(kind == 2, 8 + slot % 4, NA))
    run_part = jnp.where(kind < 2, kind, slot // 4)
    offset = jnp.zeros((1, 128), jnp.int32)
    for a in range(NA):
        offset = jnp.where(run == a, panel[64 * a + pos[1]], offset)
    col = jnp.where(run < NA, STRIDE * run + offset, -1)
    rows = lax.broadcasted_iota(jnp.int32, (96, 128), 0)
    total = jnp.zeros((128, 128), F32)
    for z in range(NZ):
        for part in range(2):
            chosen = ((rows == col) & (run_part == part) & (run_z == z)).astype(F32).astype(BF16)
            total += lax.dot_general(
                rec[part, :, 128 * z : 128 * z + 128],
                chosen,
                (((0,), (0,)), ((), ())),
                preferred_element_type=F32,
            )
    to_rcv[...] = total.astype(BF16).reshape(NP, 8, 128)


def turned(x, shift):
    return pltpu.roll(x, shift % 128, 1) if shift % 128 else x


def order_behind_kernel(from_src, behind):
    lane = lax.broadcasted_iota(jnp.int32, (8, 128), 1)
    tiles = [from_src[a].astype(F32) for a in range(NA)]
    for part in range(2):
        for pair in range(2):
            for kind in range(2):
                acc = jnp.zeros((8, 128), F32)
                for a in range(8):
                    acc = jnp.where(lane % 8 == a, turned(tiles[a], a - (4 * part + 2 * pair + kind)), acc)
                behind[6 * part + 3 * pair + kind] = acc.astype(BF16)
            acc = jnp.zeros((8, 128), F32)
            for odd in range(2):
                for a in range(8, NA):
                    shift = 64 * (odd - part) + a - 8 - (2 * pair + odd)
                    acc = jnp.where((lane // 64 == odd) & (lane % 4 == a - 8), turned(tiles[a], shift), acc)
            behind[6 * part + 3 * pair + 2] = acc.astype(BF16)


def order_kernel(from_rcv, behind, out):
    pos = position()
    lane = lax.broadcasted_iota(jnp.int32, (8, 128), 1)
    tiles = [from_rcv[p].astype(F32) for p in range(NP)]
    odd = pos[1] // NP % 2 == 1
    for z in range(NZ):
        for kind in range(3):
            acc = jnp.zeros((8, 128), F32)
            for p in range(NP):
                if kind < 2:
                    acc = jnp.where(lane // 8 == p, turned(tiles[p], 8 * p - 32 * z - 8 * kind), acc)
                else:
                    for part in range(2):
                        shift = 64 * part + 4 * p - 32 * z - 16 - 4 * part
                        acc = jnp.where(lane // 4 == 16 * part + p, turned(tiles[p], shift), acc)
            if kind == 2:
                acc = jnp.where(odd, pltpu.roll(acc, 64, 1), acc)
            tile = acc.astype(BF16)
            for copy in range(NZ):
                out[copy, 3 * z + kind] = tile
    for copy in range(NZ):
        out[copy, TILES:] = behind[...]


def average_kernel(pieces, out, own, rows, sems):
    low = lax.broadcasted_iota(jnp.int32, (8, 128), 1) < 64
    for z in range(NZ):
        for tile in range(TILES):
            part, pair, kind = tile // 6, tile % 6 // 3, tile % 3
            if kind < 2:
                front = pieces[2 * pair + kind, 3 * z + part].astype(F32)
            else:
                even, odd = [pieces[2 * pair + n, 3 * z + 2].astype(F32) for n in range(2)]
                front = pltpu.roll(jnp.where(low, odd, even), 64, 1) if part else jnp.where(low, even, odd)
            rows[z, tile] = ((front + pieces[z, TILES + tile].astype(F32)) * 0.5).astype(BF16)
    copies = [pltpu.make_async_copy(rows, out.at[n], sems.at[n]) for n in range(NY)]
    for copy in copies:
        copy.start()
    own[...] = rows[position()[1] // NP]
    for copy in copies:
        copy.wait()


def widen_kernel(rec, next_src, last_src, wide):
    lane = lax.broadcasted_iota(jnp.int32, (8, 128), 1)
    for part in range(2):
        for a in range(NA):
            run = slice(8 * a, 8 * a + 8)
            for n in range(EXT // 128 - 1):
                wide[part, a, n] = rec[part, run, 128 * n : 128 * n + 128]
            after, before = next_src[part, run].astype(F32), last_src[part, run].astype(F32)
            rim = jnp.where(lane < 8, after, jnp.where(lane >= 120, before, jnp.zeros_like(before)))
            wide[part, a, EXT // 128 - 1] = rim.astype(BF16)


def bounds(rcv):
    return (rcv == 0).astype(jnp.int32), (rcv == NZ * NP - 1).astype(jnp.int32)


def sides(core, partner, beyond):
    return jnp.where(core == 0, beyond, partner), jnp.where(core == 0, partner, beyond)


def neighbours(a, first, last):
    keep_lo = (a - first >= 0).astype(F32)
    keep_hi = (a + last <= NA - 1).astype(F32)
    return jnp.maximum(a - first, 0), jnp.minimum(a + last, NA - 1), keep_lo, keep_hi


def windows_rows(x, count):
    two = x[:-1] + x[1:]
    four = two[:-2] + two[2:]
    eight = four[:-4] + four[4:]
    return eight[:count] + x[8 : 8 + count]


def windows_lanes(source, target, band, pairs):
    count = EXT // 128
    rows = source.shape[0] * source.shape[1] * source.shape[2]
    tiles = []
    for n in range(count):
        x = source[:, :, :, 128 * n : 128 * n + 128].reshape(rows, 128)
        high = x.astype(BF16)
        tiles.append((high, (x - high.astype(F32)).astype(BF16)))
    for n in pairs:
        width = min(2, count - n)
        total = jnp.zeros((rows, 128 * width), F32)
        for half in range(2):
            near = jnp.concatenate([tiles[(n + m) % count][half] for m in range(-1, width + 1)], axis=1)
            total += jnp.dot(near, band[: 128 * (width + 2), : 128 * width], preferred_element_type=F32)
        target[:, :, :, 128 * n : 128 * (n + width)] = total.reshape(*target.shape[:3], 128 * width)


def place(a):
    src = position()[0]
    return 4 * ((src + 3 - a % 3) % 3) + (src // 3 + 4 - a // 3) % 4


def halves(a_rows):
    left = a_rows[...].reshape(a_rows.shape[0] * a_rows.shape[1], 128 * TILES)
    return left[:, : 64 * TILES], left[:, 64 * TILES :]


def times(x, y):
    return lax.dot_general(x, y, (((1,), (1,)), ((), ())), preferred_element_type=F32)


def products(a_rows, b_rows, guess):
    left = halves(a_rows)
    values = []
    for n in range(NZ // 2):
        cols = slice(256 * n, 256 * n + 256)
        right = b_rows[cols, : 64 * TILES], b_rows[cols, 64 * TILES :]
        value = (
            times(left[0], right[0]) - times(left[1], right[1]),
            times(left[0], right[1]) + times(left[1], right[0]),
        )
        values.append([v.reshape(*a_rows.shape[:2], 256) for v in value])
        for part in range(2):
            guess[part, :, :, cols] = values[-1][part].astype(BF16)
    return values


def predict_kernel(sr, partner, ss, sp, guess, mult, a_rows, b_rows):
    core = position()[1] % 2

    def spread(a, _):
        for t in range(TILES):
            x = jnp.concatenate([sr[place(a), t].astype(F32), partner[place(a), t].astype(F32)], axis=0)
            a_rows[a, :, 128 * t : 128 * t + 128] = x.astype(BF16)
        return 0

    lax.fori_loop(0, NA, spread, 0, unroll=2)
    for z in range(NZ):
        for t in range(TILES):
            mine, theirs = ss[:, z, t].astype(F32), sp[:, z, t].astype(F32)
            zero = jnp.where(core == 0, mine, theirs)
            one = jnp.where(core == 0, theirs, mine)
            x = jnp.stack([zero, one], axis=1).reshape(128, 128)
            b_rows[128 * z : 128 * z + 128, 128 * t : 128 * t + 128] = x.astype(BF16)
    for n, value in enumerate(products(a_rows, b_rows, guess)):
        for part in range(2):
            mult[part, :, :, 256 * n : 256 * n + 256] = (value[part][:, :8] * (768.0 ** -0.5)).astype(BF16)


def predict_far_kernel(beyond, b_rows, guess, a_rows):
    rcv = position()[1]
    first, last = bounds(rcv)

    def spread(a, _):
        lo, hi, keep_lo, keep_hi = neighbours(a, first, last)
        run, keep = jnp.where(rcv % 2 == 0, lo, hi), jnp.where(rcv % 2 == 0, keep_lo, keep_hi)
        for t in range(TILES):
            a_rows[a, :, 128 * t : 128 * t + 128] = (beyond[place(run), t].astype(F32) * keep).astype(BF16)
        return 0

    lax.fori_loop(0, NA, spread, 0, unroll=2)
    products(a_rows, b_rows, guess)


def subtract_kernel(wide, partner, beyond, near, far, near_rows, far_rows, row_same, row_cross, prim, data, guess, edge, edge_far, once, box):
    rcv = position()[1]
    first, last = bounds(rcv)
    rims = [(row_same[t].astype(F32), row_cross[t].astype(F32)) for t in range(TILES)]
    row_hi = [jnp.where(rcv % 2 == 0, same, cross) for same, cross in rims]
    row_lo = [jnp.where(rcv % 2 == 0, cross, same) for same, cross in rims]
    right = []
    for part in range(2):
        tiles = range(6 * part, 6 * part + 6)
        right.append(
            jnp.concatenate(
                [
                    jnp.concatenate([row_hi[t] for t in tiles], axis=1),
                    jnp.zeros((112, 64 * TILES), F32),
                    jnp.concatenate([row_lo[t] for t in tiles], axis=1),
                ],
                axis=0,
            ).astype(BF16)
        )
    for a_rows, target in ((near_rows, edge), (far_rows, edge_far)):
        left = halves(a_rows)
        straight = times(left[0], jnp.concatenate(right, axis=0))
        crossed = times(left[1], jnp.concatenate(right[::-1], axis=0))
        real, imag = straight[:, :128] - crossed[:, :128], straight[:, 128:] + crossed[:, 128:]
        target[0] = real.astype(BF16).astype(F32).reshape(*a_rows.shape[:2], 128)
        target[1] = imag.astype(BF16).astype(F32).reshape(*a_rows.shape[:2], 128)

    def run_of(ref, part, a):
        return jnp.concatenate([ref[part, a, n].astype(F32) for n in range(EXT // 128)], axis=1)

    def guess_of(part, a):
        inner = jnp.concatenate([near[part, a].astype(F32), edge[part, a]], axis=1)
        outer = jnp.concatenate([far[part, a].astype(F32), edge_far[part, a]], axis=1)
        below, above = sides(rcv % 2, inner[8:], outer)
        return jnp.concatenate([below, inner[:8], above], axis=0)

    def terms_of(dr, di, pr, pi):
        return pr * dr + pi * di, pr * di - pi * dr, pr * pr + pi * pi

    def subtract(dr, di, pr, pi, sums):
        den = sums[2] + EPS
        gain_re, gain_im = sums[0] / den, sums[1] / den
        return dr - (gain_re * pr - gain_im * pi), di - (gain_re * pi + gain_im * pr)

    def first_sweep(a, _):
        lo, hi, keep_lo, keep_hi = neighbours(a, first, last)
        for part in range(2):
            below, _ = sides(rcv % 2, run_of(partner, part, lo), run_of(beyond, part, lo))
            _, above = sides(rcv % 2, run_of(partner, part, hi), run_of(beyond, part, hi))
            data[part, a] = jnp.concatenate([below * keep_lo, run_of(wide, part, a), above * keep_hi], axis=0)
            guess[part, a] = guess_of(part, a)
        dr, di = data[0, a], data[1, a]
        weight = 1.5 - jnp.tanh(dr * dr + di * di)
        for n, q in enumerate(terms_of(dr, di, guess[0, a], guess[1, a])):
            once[n, a] = windows_rows(weight * q, 16)
        return 0

    lax.fori_loop(0, NA, first_sweep, 0, unroll=2)
    far = lax.broadcasted_iota(jnp.int32, (512, 256), 0) - lax.broadcasted_iota(jnp.int32, (512, 256), 1) - 128
    band = (jnp.abs(far) <= REACH).astype(F32).astype(BF16)
    windows_lanes(once, box, band, (0, 2, 4))

    def second_sweep(a, _):
        dr, di = data[0, a, 4:20], data[1, a, 4:20]
        pr, pi = guess[0, a, 4:20], guess[1, a, 4:20]
        er, ei = subtract(dr, di, pr, pi, [box[n, a] for n in range(3)])
        again = 1.5 - jnp.tanh(er * er + ei * ei)
        for n, q in enumerate(terms_of(dr, di, pr, pi)):
            once[n, a, :8] = windows_rows(again * q, 8)
        return 0

    lax.fori_loop(0, NA, second_sweep, 0, unroll=2)
    windows_lanes(once.at[:, :, :8], box.at[:, :, :8], band, (0, 2))

    def finish(a, _):
        dr, di = [data[part, a, 8:16, :512] for part in range(2)]
        pr, pi = [guess[part, a, 8:16, :512] for part in range(2)]
        er, ei = subtract(dr, di, pr, pi, [box[n, a, :8, :512] for n in range(3)])
        prim[0, a], prim[1, a] = er.astype(BF16), ei.astype(BF16)
        return 0

    lax.fori_loop(0, NA, finish, 0, unroll=2)


def shape(*dims):
    return jax.ShapeDtypeStruct(dims, BF16)


def ring(count, step, closed):
    return [(n, (n + step) % count) for n in range(count) if closed or 0 <= n + step < count]


def block(record, panel_offset):
    src_count, rcv_count = lax.axis_size("src"), lax.axis_size("rcv")
    rec = record[0]
    plane = [[z * NP + p for p in range(NP)] for z in range(NZ)]
    column = [[z * NP + p for z in range(NZ)] for p in range(NP)]
    line = [[z * NP + y * NC + c for y in range(NY)] for z in range(NZ) for c in range(NC)]
    swap = [(n, n ^ 1) for n in range(rcv_count)]
    beyond = [(n, (n + (1 if n % 2 else -1)) % rcv_count) for n in range(rcv_count)]

    def exchange(x, axis, groups=None):
        return lax.all_to_all(x, axis, split_axis=0, concat_axis=0, tiled=True, axis_index_groups=groups)

    def kernel(body, outs, scalars, arrays, scratch=(), flops=1 << 20, limit=8 << 20, spaces=None):
        spaces = spaces or jax.tree.map(lambda _: pltpu.VMEM, outs)
        return pl.pallas_call(
            body,
            out_shape=outs,
            in_specs=smem(len(scalars)) + vmem(len(arrays)),
            out_specs=jax.tree.map(lambda m: pl.BlockSpec(memory_space=m), spaces),
            scratch_shapes=scratch,
            compiler_params=pltpu.CompilerParams(vmem_limit_bytes=limit),
            cost_estimate=pl.CostEstimate(flops=flops, bytes_accessed=1 << 20, transcendentals=0),
        )(*scalars, *arrays)

    to_src = kernel(pick_behind_kernel, shape(NA, 8, 128), (panel_offset,), (rec,), limit=60 << 20)
    from_src = exchange(to_src, "src")
    to_rcv = kernel(pick_front_kernel, shape(NP, 8, 128), (panel_offset,), (rec,))
    from_rcv = exchange(to_rcv, "rcv", plane)
    behind = kernel(order_behind_kernel, shape(TILES, 8, 128), (), (from_src,))
    message = kernel(order_kernel, shape(NZ, 2 * TILES, 8, 128), (), (from_rcv, behind))
    pieces = exchange(message, "rcv", column)
    held, _ = lax.optimization_barrier((rec, from_src))
    first_tile, last_tile = held[:, :, :128], held[:, :, 384:]
    next_src = lax.ppermute(first_tile, "src", ring(src_count, -1, False))
    last_src = lax.ppermute(last_tile, "src", ring(src_count, 1, False))
    wide = kernel(widen_kernel, shape(2, NA, EXT // 128, 8, 128), (), (rec, next_src, last_src))
    wide_beyond = lax.ppermute(wide, "rcv", beyond)
    wide_partner = lax.ppermute(wide, "rcv", swap)
    spread, own = kernel(
        average_kernel,
        (shape(NY, NZ, TILES, 8, 128), shape(TILES, 8, 128)),
        (),
        (pieces,),
        [pltpu.VMEM((NZ, TILES, 8, 128), BF16), pltpu.SemaphoreType.DMA((NY,))],
        spaces=(pltpu.HBM, pltpu.VMEM),
    )
    ss = exchange(spread, "rcv", line)
    moved = [lax.ppermute(own, "src", ring(src_count, 3 * d, True)) for d in range(1, 4)]
    sr = jnp.stack([own, *moved])
    moved = [
        lax.ppermute(sr, "src", [(n, n - n % 3 + (n + e) % 3) for n in range(src_count)]) for e in range(1, 3)
    ]
    sr = jnp.concatenate([sr, *moved])
    sr_beyond = lax.ppermute(sr, "rcv", beyond)
    sr_partner = lax.ppermute(sr, "rcv", swap)
    row = jnp.where(lax.axis_index("rcv") % 2 == 0, ss[0, 0], ss[NY - 1, NZ - 1])
    same, cross = [
        [
            (n * rcv_count + k, to * rcv_count + (k ^ flip))
            for n in range(src_count)
            for k in range(rcv_count)
            for to in (n + (1 if k % 2 else -1),)
            if 0 <= to < src_count
        ]
        for flip in range(2)
    ]
    row_same = lax.ppermute(row, ("src", "rcv"), same)
    row_cross = lax.ppermute(row, ("src", "rcv"), cross)
    sp = lax.ppermute(ss, "rcv", swap)
    wide_rows = (512, 128 * TILES)
    guess, mult, left, right = kernel(
        predict_kernel,
        (shape(2, NA, 16, 512), shape(2, NA, 8, 512), shape(NA, 16, 128 * TILES), shape(*wide_rows)),
        (),
        (sr, sr_partner, ss, sp),
        flops=1 << 32,
        limit=16 << 20,
    )
    guess_far, left_far = kernel(
        predict_far_kernel,
        (shape(2, NA, 8, 512), shape(NA, 8, 128 * TILES)),
        (),
        (sr_beyond, right),
        flops=1 << 31,
        limit=12 << 20,
    )
    prim = kernel(
        subtract_kernel,
        shape(2, NA, 8, 512),
        (),
        (wide, wide_partner, wide_beyond, guess, guess_far, left, left_far, row_same, row_cross),
        [
            pltpu.VMEM((2, NA, 24, EXT), F32),
            pltpu.VMEM((2, NA, 24, EXT), F32),
            pltpu.VMEM((2, NA, 16, 128), F32),
            pltpu.VMEM((2, NA, 8, 128), F32),
            pltpu.VMEM((3, NA, 16, EXT), F32),
            pltpu.VMEM((3, NA, 16, EXT), F32),
        ],
        flops=1 << 32,
        limit=24 << 20,
    )
    return prim.reshape(record.shape), mult.reshape(record.shape)


def solution(mesh):
    in_specs = (P(None, None, "rcv", "src"), P())
    out_specs = (P(None, None, "rcv", "src"), P(None, None, "rcv", "src"))
    return jax.shard_map(block, mesh=mesh, in_specs=in_specs, out_specs=out_specs, check_vma=False)
```
